32 devices in a mesh: vessel: 2 (over core), gather: 16 (over z, y, x).
Axes of the slice: x: 2, y: 2, z: 4, core: 2. Of those that a mesh axis runs over, the one named last changes fastest.
Arguments:
- observed: bfloat16 [16, 16, 2048], P('gather'), may hold values from -6 to 6
- estimate: bfloat16 [2, 16, 16, 2048], P('vessel', 'gather'), may hold values from -6 to 6
- delays: int32 [2, 16], P('vessel', 'gather'), may hold values from 0 to 256
- taps_time: float32 [16, 7], replicated, may hold values from -2 to 2
- taps_shot: float32 [16, 7], replicated, may hold values from -0.5 to 0.5
- thresh: float32 [16], replicated, may hold values from 0.02 to 0.3
Outputs:
- deblended: bfloat16 [2, 16, 16, 2048], P('vessel', 'gather')
The draws below stay inside these ranges and needn't reach their ends.
All inputs are finite; a program needn't handle non-finite values.
Results may differ from the reference program's by a relative error of at most 0.022.
Values may be sent and summed in bfloat16 or wider, within the bound.
A program may use at most 64 MiB of HBM per device.

```python
import math
import jax
import jax.numpy as jnp
from jax import lax

TT = 2048
CH = 16
TAPS = 7
TIME_SPACING = 4
SHOT_SPACING = 2
MAXD = 256
ITERS = 2
VES = 2
SHOTS = 16
REC = 16


def with_ends(array, rng, least, largest):
    extent = array.shape
    spot = [jax.random.randint(jax.random.fold_in(rng, axis), (), 0, extent[axis]) for axis in range(len(extent))]
    array = array.at[tuple(spot)].set(least)
    longest = extent.index(max(extent))
    spot[longest] = (spot[longest] + 1) % extent[longest]
    return array.at[tuple(spot)].set(largest)


def block_scale(key, shape, shards, smallest, largest):
    gain = 1.0
    for axis_at, blocks in shards:
        draws = jax.random.uniform(jax.random.fold_in(jax.random.fold_in(key, 6), axis_at), (blocks,), jnp.float32, smallest / len(shards), largest / len(shards))
        gain = gain * jnp.repeat(jnp.exp(draws), shape[axis_at] // blocks).reshape((-1,) + (1,) * (len(shape) - 1 - axis_at))
    return gain


def scatter_about(stream_key, dims, deviation, most, shards=(), held_as=jnp.bfloat16):
    loudness = block_scale(stream_key, dims, shards, -0.22, 0.18) if shards else 1.0
    result = jax.random.normal(stream_key, dims, jnp.float32) * deviation * loudness
    return jnp.minimum(jnp.maximum(result, -most), most).astype(held_as)


def setup_inputs(seed: int = 0) -> dict:
    keys = jax.random.split(jax.random.key(seed), 7)
    observed = scatter_about(keys[0], (SHOTS, REC, TT), 1.0, 6.0, ((0, 16),))
    estimate = scatter_about(keys[1], (VES, SHOTS, REC, TT), 0.7, 6.0, ((0, 2), (1, 16)))
    delays = with_ends(jax.random.randint(keys[2], (VES, SHOTS), 0, MAXD + 1), jax.random.fold_in(keys[2], 1), 0, MAXD).astype(jnp.int32)
    taps_time = scatter_about(keys[3], (CH, TAPS), TAPS ** -0.5, 2.0, (), jnp.float32)
    taps_shot = scatter_about(keys[4], (CH, TAPS), (TAPS * CH) ** -0.5, 0.5, (), jnp.float32)
    thresh = jnp.clip(jnp.exp(jax.random.uniform(keys[5], (CH,), jnp.float32, math.log(0.02), math.log(0.3))), 0.02, 0.3)
    return {"observed": observed, "estimate": estimate, "delays": delays, "taps_time": taps_time, "taps_shot": taps_shot, "thresh": thresh}


def late_shift(traces, shift_by):
    padded = jnp.pad(traces, ((0, 0), (0, 0), (MAXD, MAXD)))

    def single(trace, shift_amount):
        return lax.dynamic_slice_in_dim(trace, (MAXD - shift_amount).astype(jnp.int32), TT, 1)

    return jax.vmap(single)(padded, shift_by)


def early_shift(traces, shift_by):
    padded = jnp.pad(traces, ((0, 0), (0, 0), (MAXD, MAXD)))

    def single(trace, shift_amount):
        return lax.dynamic_slice_in_dim(trace, (MAXD + shift_amount).astype(jnp.int32), TT, 1)

    return jax.vmap(single)(padded, shift_by)


def along_time(field, taps, shift_sign):
    filter_reach = 3 * TIME_SPACING
    length = field.shape[3]
    padded = jnp.pad(field, ((0, 0), (0, 0), (0, 0), (filter_reach, filter_reach)))
    total = jnp.zeros((taps.shape[0],) + field.shape[1:], jnp.float32)
    for tap_index in range(-3, 4):
        start_offset = filter_reach + shift_sign * tap_index * TIME_SPACING
        total = total + taps[:, tap_index + 3][:, None, None, None] * padded[:, :, :, start_offset:start_offset + length]
    return total


def along_shots(field, taps, shift_sign):
    filter_reach = 3 * SHOT_SPACING
    length = field.shape[1]
    padded = jnp.pad(field, ((0, 0), (filter_reach, filter_reach), (0, 0), (0, 0)))
    total = jnp.zeros((taps.shape[0],) + field.shape[1:], jnp.float32)
    for tap_index in range(-3, 4):
        start_offset = filter_reach + shift_sign * tap_index * SHOT_SPACING
        total = total + taps[:, tap_index + 3][:, None, None, None] * padded[:, start_offset:start_offset + length]
    return total


def shrink_filter(plane, taps_time, taps_shot, thresh):
    field = plane.astype(jnp.float32)[None]
    group_time = taps_time.reshape(-1, 4, taps_time.shape[1])
    group_shot = taps_shot.reshape(-1, 4, taps_shot.shape[1])
    group_thresh = thresh.reshape(-1, 4)

    def channel(carry, pieces):
        time_taps, shot_taps, limits = pieces
        forward_pass = along_shots(along_time(field, time_taps, 1), shot_taps, 1)
        bound = limits[:, None, None, None]
        shrunk = forward_pass - jnp.clip(forward_pass, -bound, bound)
        back = along_time(along_shots(shrunk, shot_taps, -1), time_taps, -1)
        return carry + jnp.sum(back, axis=0), None

    total, _ = lax.scan(channel, jnp.zeros(plane.shape, jnp.float32), (group_time, group_shot, group_thresh))
    return total.astype(jnp.bfloat16)


def reference(observed, estimate, delays, taps_time, taps_shot, thresh):
    current = estimate
    for step in range(ITERS):
        blend = jnp.zeros(observed.shape, jnp.float32)
        for vessel_index in range(VES):
            blend = blend + late_shift(current[vessel_index], delays[vessel_index]).astype(jnp.float32)
        resid = observed.astype(jnp.float32) - blend
        updated = []
        for vessel_index in range(VES):
            plane = (current[vessel_index].astype(jnp.float32) + early_shift(resid, delays[vessel_index])).astype(jnp.bfloat16)
            updated.append(shrink_filter(plane, taps_time, taps_shot, thresh))
        current = jnp.stack(updated)
    return current
```

```python
import functools

import jax
import jax.numpy as jnp
from jax import lax
from jax.experimental import pallas as pl
from jax.experimental.pallas import tpu as pltpu
from jax.sharding import PartitionSpec as P

TIME_SPACING = 4
SHOT_SPACING = 2
MAXD = 256
ITERS = 2
LANES = 128
REACH = 3
SIDE = 8

MESH = pl.DeviceIdType.MESH


def partner_of(me, i, n):
    return me ^ (n - i) if n & (n - 1) == 0 else lax.rem(me + i, n)


def across(column, extent):
    return jnp.concatenate([column] * (extent // LANES), axis=1)


def lane_of(shape):
    return lax.broadcasted_iota(jnp.int32, shape, 1)


def shift_rows(tiles, amount, count, most):
    shape = amount.shape
    zero = jnp.zeros(shape, jnp.float32)
    within = amount & (LANES - 1)
    whole = amount >> (LANES.bit_length() - 1)
    reach = lane_of(shape) + within
    index = reach & (LANES - 1)
    wrapped = reach >= LANES
    extent = count + most + 1
    tiles = list(tiles) + [None] * (extent - len(tiles))
    turned = [None if t is None else jnp.take_along_axis(t, index, axis=1, mode="promise_in_bounds") for t in tiles]

    def pick(mask, a, b):
        if a is None and b is None:
            return None
        return jnp.where(mask, zero if a is None else a, zero if b is None else b)

    level = [pick(wrapped, turned[j + 1], turned[j]) for j in range(extent - 1)]
    step = 1
    while step <= most:
        mask = (whole & step) != 0
        level = [
            pick(mask, level[j + step] if j + step < len(level) else None, level[j]) for j in range(len(level))
        ]
        step *= 2
    return [zero if t is None else t for t in level[:count]]


def kernel(
    dims,
    x_hbm,
    obs_hbm,
    d_hbm,
    tt_hbm,
    ts_hbm,
    th_hbm,
    out_ref,
    x_ref,
    obs_ref,
    tt_ref,
    ts_ref,
    th_ref,
    s_in,
    flat,
    flat2,
    side_flat,
    side,
    side_buf,
    stage,
    rbuf,
    seen,
    seen_buf,
    stage2,
    rbuf2,
    d_mine,
    d_other,
    m_s,
    mt_s,
    th_s,
    plane_s,
    pst,
    g_s,
    tail_s,
    tail_r,
    s_side,
    r_side,
    s_pay,
    r_pay,
    s_seen,
    r_seen,
    s_del,
    r_del,
    s_tail,
    r_tail,
    s_out,
    r_out,
):
    n, width, channels, taps, chunks, rows, depth = dims
    v = lax.axis_index("vessel")
    me = lax.axis_index("gather")
    other = 1 - v
    nt = width // LANES
    group = rows // n
    f32, bf16 = jnp.float32, jnp.bfloat16

    loads = [
        pltpu.make_async_copy(source, target, s_in.at[i])
        for i, (source, target) in enumerate(
            (
                (x_hbm.at[0, 0], x_ref),
                (obs_hbm.at[0], obs_ref),
                (tt_hbm, tt_ref),
                (ts_hbm, ts_ref),
                (th_hbm, th_ref),
            )
        )
    ]
    for load in loads[:2]:
        load.start()

    barrier = pltpu.get_barrier_semaphore()

    def greet(i, carry):
        p = partner_of(me, i, n)
        pl.semaphore_signal(barrier, inc=1, device_id=(v, p), device_id_type=MESH)
        pl.semaphore_signal(barrier, inc=1, device_id=(other, p), device_id_type=MESH)
        return carry

    lax.fori_loop(1, n, greet, 0)
    pl.semaphore_signal(barrier, inc=1, device_id=(other, me), device_id_type=MESH)
    for load in loads[2:]:
        load.start()

    side_flat[...] = jnp.zeros((n * SIDE, LANES), f32)
    plane_s[:, :LANES] = jnp.zeros((n, LANES), bf16)
    plane_s[:, LANES + width :] = jnp.zeros((n, LANES), bf16)
    if depth > taps * n:
        pst[taps * n :, :] = jnp.zeros((depth - taps * n, width), bf16)

    def put(ref, i, stride, value):
        ref[pl.ds(i, n, stride=stride), :] = value

    def take(ref, i, stride):
        return ref[pl.ds(i, n, stride=stride), :]

    def tiles_of(ref):
        return [ref[:, i * LANES : (i + 1) * LANES].astype(f32) for i in range(nt)]

    for load in loads[:2]:
        load.wait()
    d = jnp.full((n, LANES), d_hbm[0, 0], jnp.int32)
    lane = lane_of((n, LANES))
    most = MAXD // LANES

    put(side_flat, 0, SIDE, d.astype(f32))
    tiles = tiles_of(x_ref)
    for j in range(most):
        put(side_flat, 2 + j, SIDE, tiles[nt - most + j])
    side[...] = side_flat[...].reshape(n, SIDE, LANES).astype(bf16)
    moved = shift_rows([None] * most + tiles, MAXD - d, nt, most)
    tiles = tiles_of(obs_ref)
    for i in range(nt):
        put(flat, i, nt, tiles[i] - moved[i])
    stage[...] = flat[...].reshape(n, nt, LANES).astype(bf16)

    pl.semaphore_wait(barrier, 2 * n - 1)

    def hand(src, dst, send_sem, recv_sem, vessel, p):
        return pltpu.make_async_remote_copy(
            src_ref=src,
            dst_ref=dst,
            send_sem=send_sem,
            recv_sem=recv_sem,
            device_id=(vessel, p),
            device_id_type=MESH,
        )

    def batch(src, dst, send_sem, recv_sem, vessel, count):
        def one(p):
            return hand(src.at[p], dst.at[me], send_sem, recv_sem, vessel, p)

        return one, hand(src.at[pl.ds(0, count)], dst.at[pl.ds(0, count)], send_sem, recv_sem, vessel, me)

    cross, all_cross = batch(side, side_buf, s_side, r_side, other, n)
    payload, all_payload = batch(stage, rbuf, s_pay, r_pay, v, n - 1)
    later, all_later = batch(seen, seen_buf, s_seen, r_seen, v, n - 1)
    result, all_result = batch(stage2, rbuf2, s_out, r_out, v, n - 1)

    def to_all(copy):
        def send(i, carry):
            copy(partner_of(me, i, n)).start()
            return carry

        lax.fori_loop(1, n, send, 0)

    to_all(cross)
    to_all(payload)
    cross(me).start()
    rbuf[me] = stage[me]

    moved = shift_rows(tiles_of(obs_ref), d, nt, most)
    for i in range(nt):
        put(flat2, i, nt, moved[i])
    seen[...] = flat2[...].reshape(n, nt, LANES).astype(bf16)
    to_all(later)
    seen_buf[me] = seen[me]

    for load in loads[2:]:
        load.wait()

    def build(q, carry):
        row_ch = q * group + lax.broadcasted_iota(jnp.int32, (rows, channels), 0) // n
        pick = row_ch == lax.broadcasted_iota(jnp.int32, (rows, channels), 1)
        pick_f = pick.astype(f32)
        tt = lax.dot_general(pick_f, tt_ref[...], (((1,), (1,)), ((), ())), precision=lax.Precision.HIGHEST, preferred_element_type=f32)
        ts = lax.dot_general(pick_f, ts_ref[...], (((1,), (1,)), ((), ())), precision=lax.Precision.HIGHEST, preferred_element_type=f32)
        th_s[q] = jnp.broadcast_to(jnp.sum(jnp.where(pick, th_ref[...], 0.0), axis=1, keepdims=True), (rows, LANES))
        col = lax.broadcasted_iota(jnp.int32, (rows, depth), 1)
        row = lax.broadcasted_iota(jnp.int32, (rows, depth), 0)
        apart = lax.rem(col, n) - lax.rem(row, n)
        tap_of = col // n
        a = jnp.zeros((rows, depth), f32)
        b = jnp.zeros((rows, depth), f32)
        for k in range(taps):
            a = jnp.where(tap_of == k, tt[:, k : k + 1], a)
            b = jnp.where(apart == (k - REACH) * SHOT_SPACING, ts[:, k : k + 1], b)
        m = a * b
        m_s[q] = m.astype(bf16)
        mt_s[q] = m.T.astype(bf16)
        return carry

    if chunks == 1:
        build(0, 0)
    else:
        lax.fori_loop(0, chunks, build, 0)

    block_width = 2048

    def filter_columns(start, stop):
        def one(q, first):
            for c0 in range(start, stop, block_width):
                c1 = min(c0 + block_width, stop)
                y = jnp.dot(m_s[q], pst[:, c0:c1], preferred_element_type=f32)
                th = across(th_s[q], c1 - c0)
                z = (y - jnp.minimum(jnp.maximum(y, -th), th)).astype(bf16)
                g = jnp.dot(mt_s[q], z, preferred_element_type=f32)
                if first:
                    g_s[:, c0:c1] = g
                else:
                    g_s[:, c0:c1] += g

        one(0, True)
        if chunks > 1:

            def more(q, carry):
                one(q, False)
                return carry

            lax.fori_loop(1, chunks, more, 0)

    def stack_taps(start, stop):
        lo = start
        piece = plane_s[:, lo : stop + 2 * LANES]
        extent = piece.shape[1]
        for k in range(taps):
            step = (k - REACH) * TIME_SPACING
            moved = piece if step == 0 else pltpu.roll(piece, (extent - step) % extent, 1)
            pst[k * n : (k + 1) * n, start:stop] = moved[:, LANES : LANES + stop - start]

    def collect():
        total = jnp.zeros((n, width), f32)
        for k in range(taps):
            step = (k - REACH) * TIME_SPACING
            g = g_s[k * n : (k + 1) * n, :]
            if step != 0:
                extent = width + LANES
                g = pltpu.roll(jnp.concatenate([g, jnp.zeros((n, LANES), f32)], axis=1), step % extent, 1)[:, :width]
            total = total + g
        return total.astype(bf16)

    def store_plane(i, value):
        plane_s[:, LANES + i * LANES : LANES + (i + 1) * LANES] = value.astype(bf16)

    cut = nt - most

    def before_end(i, delay):
        return i * LANES + lane + delay < width

    all_cross.wait_recv()
    side_flat[...] = side_buf[...].astype(f32).reshape(n * SIDE, LANES)
    theirs = take(side_flat, 0, SIDE).astype(jnp.int32)
    d_other[...] = theirs
    swap = hand(d_other, d_mine, s_del, r_del, other, me)
    swap.start()

    all_payload.wait_recv()
    flat[...] = rbuf[...].astype(f32).reshape(n * nt, LANES)
    moved = shift_rows([take(flat, i, nt) for i in range(nt)], theirs, nt, most)
    for i in range(nt):
        value = moved[i]
        if i >= cut:
            value = jnp.where(before_end(i, theirs), value, take(side_flat, 2 + i - cut, SIDE))
        store_plane(i, value)
    stack_taps(0, width)
    filter_columns(0, width)
    held = collect()
    tail_s[...] = held[:, width - MAXD :]
    trade = hand(tail_s, tail_r, s_tail, r_tail, other, me)
    trade.start()
    all_later.wait_recv()
    swap.wait_recv()
    flat2[...] = seen_buf[...].astype(f32).reshape(n * nt, LANES)
    ours = d_mine[...]
    tiles = [None] * most + [held[:, i * LANES : (i + 1) * LANES].astype(f32) for i in range(nt)]
    moved = shift_rows(tiles, ours - theirs + MAXD, nt, 2 * most)
    for i in range(cut):
        store_plane(i, take(flat2, i, nt) - moved[i])
    trade.wait_recv()
    for i in range(cut, nt):
        end = tail_r[:, (i - cut) * LANES : (i - cut + 1) * LANES].astype(f32)
        store_plane(i, jnp.where(before_end(i, ours), take(flat2, i, nt) - moved[i], end))
    stack_taps(0, width)
    filter_columns(0, width)
    held = collect()

    for i in range(nt):
        put(flat, i, nt, held[:, i * LANES : (i + 1) * LANES].astype(f32))
    stage2[...] = flat[...].reshape(n, nt, LANES).astype(bf16)
    to_all(result)
    rbuf2[me] = stage2[me]

    all_cross.wait_send()
    all_payload.wait_send()
    all_later.wait_send()
    swap.wait_send()
    trade.wait_send()

    all_result.wait_recv()
    flat[...] = rbuf2[...].astype(f32).reshape(n * nt, LANES)
    for i in range(nt):
        out_ref[0, 0, :, i * LANES : (i + 1) * LANES] = take(flat, i, nt).astype(bf16)
    all_result.wait_send()


def per_device(n, observed, estimate, delays, taps_time, taps_shot, thresh):
    receivers, width = observed.shape[1:]
    channels, taps = taps_time.shape
    assert observed.shape[0] == 1 and receivers == n and width % LANES == 0
    group = max(1, min(channels, 256 // n))
    chunks = channels // group
    rows = group * n
    depth = -(-taps * n // LANES) * LANES
    nt = width // LANES
    bf16, f32 = jnp.bfloat16, jnp.float32
    vmem = pl.BlockSpec(memory_space=pltpu.VMEM)
    dma = pltpu.SemaphoreType.DMA
    operands = (estimate, observed, delays, taps_time.T, taps_shot.T, thresh.reshape(1, channels))
    operands = [o if o is delays else pltpu.with_memory_space_constraint(o, pltpu.HBM) for o in operands]
    return pl.pallas_call(
        functools.partial(kernel, (n, width, channels, taps, chunks, rows, depth)),
        out_shape=pltpu.VMEM(estimate.shape, bf16),
        in_specs=[pl.BlockSpec(memory_space=pltpu.SMEM if i == 2 else pl.ANY) for i in range(6)],
        out_specs=vmem,
        scratch_shapes=[
            pltpu.VMEM((n, width), bf16),
            pltpu.VMEM((n, width), bf16),
            pltpu.VMEM((taps, channels), f32),
            pltpu.VMEM((taps, channels), f32),
            pltpu.VMEM((1, channels), f32),
            dma((5,)),
            pltpu.VMEM((n * nt, LANES), f32),
            pltpu.VMEM((n * nt, LANES), f32),
            pltpu.VMEM((n * SIDE, LANES), f32),
            pltpu.VMEM((n, SIDE, LANES), bf16),
            pltpu.VMEM((n, SIDE, LANES), bf16),
            pltpu.VMEM((n, nt, LANES), bf16),
            pltpu.VMEM((n, nt, LANES), bf16),
            pltpu.VMEM((n, nt, LANES), bf16),
            pltpu.VMEM((n, nt, LANES), bf16),
            pltpu.VMEM((n, nt, LANES), bf16),
            pltpu.VMEM((n, nt, LANES), bf16),
            pltpu.VMEM((n, LANES), jnp.int32),
            pltpu.VMEM((n, LANES), jnp.int32),
            pltpu.VMEM((chunks, rows, depth), bf16),
            pltpu.VMEM((chunks, depth, rows), bf16),
            pltpu.VMEM((chunks, rows, LANES), f32),
            pltpu.VMEM((n, width + 2 * LANES), bf16),
            pltpu.VMEM((depth, width), bf16),
            pltpu.VMEM((depth, width), f32),
            pltpu.VMEM((n, MAXD), bf16),
            pltpu.VMEM((n, MAXD), bf16),
        ]
        + [dma(())] * 12,
        compiler_params=pltpu.CompilerParams(collective_id=0, has_side_effects=True, vmem_limit_bytes=48 << 20),
    )(*operands)


def solution(mesh):
    return jax.shard_map(
        functools.partial(per_device, mesh.shape["gather"]),
        mesh=mesh,
        in_specs=(
            P("gather", None, None),
            P("vessel", "gather", None, None),
            P("vessel", "gather"),
            P(),
            P(),
            P(),
        ),
        out_specs=P("vessel", "gather", None, None),
        check_vma=False,
    )
```

```python
import functools

import jax
import jax.numpy as jnp
from jax import lax
from jax.experimental import pallas as pl
from jax.experimental.pallas import tpu as pltpu
from jax.sharding import PartitionSpec as P

TIME_SPACING = 4
MAXD = 256
ITERS = 2
LANES = 128
REACH = 3

MESH = pl.DeviceIdType.MESH


def partner_of(me, i, n):
    return me ^ (n - i) if n & (n - 1) == 0 else lax.rem(me + i, n)


def across(column, extent):
    return jnp.concatenate([column] * (extent // LANES), axis=1)


def lane_of(shape):
    return lax.broadcasted_iota(jnp.int32, shape, 1)


def shifter(tile, amount, most):
    within = amount & (LANES - 1)
    whole = amount >> (LANES.bit_length() - 1)
    reach = lane_of(amount.shape) + within
    index = reach & (LANES - 1)
    wrapped = reach >= LANES
    steps = []
    while 1 << len(steps) < most:
        steps.append((whole & (1 << len(steps))) != 0)
    farthest = whole == most

    def pick(mask, a, b):
        if a is None and b is None:
            return None
        zero = jnp.zeros(amount.shape, jnp.float32)
        return jnp.where(mask, zero if a is None else a, zero if b is None else b)

    @functools.cache
    def turned(j):
        t = tile(j)
        return None if t is None else jnp.take_along_axis(t, index, axis=1, mode="promise_in_bounds")

    @functools.cache
    def level(depth, j):
        if depth == 0:
            return pick(wrapped, turned(j + 1), turned(j))
        return pick(steps[depth - 1], level(depth - 1, j + (1 << (depth - 1))), level(depth - 1, j))

    def value(i):
        found = pick(farthest, turned(i + most), level(len(steps), i))
        return jnp.zeros(amount.shape, jnp.float32) if found is None else found

    return value


def kernel(
    dims,
    x_hbm,
    obs_hbm,
    d_hbm,
    tt_hbm,
    ts_hbm,
    th_hbm,
    out_ref,
    x_ref,
    obs_ref,
    tt_ref,
    ts_ref,
    th_ref,
    s_in,
    flat,
    stage,
    rbuf,
    flat2,
    stage2,
    rbuf2,
    flat3,
    stage3,
    rbuf3,
    m_s,
    mt_s,
    th_s,
    plane_s,
    pst,
    g_s,
    s_pay,
    r_pay,
    s_late,
    r_late,
    s_out,
    r_out,
):
    n, width, channels, taps, chunks, rows, depth = dims
    v = lax.axis_index("vessel")
    me = lax.axis_index("gather")
    other = 1 - v
    nt = width // LANES
    group = rows // n
    f32, bf16 = jnp.float32, jnp.bfloat16
    half = n // 2
    most = MAXD // LANES
    parity = lax.rem(me, 2)
    mine = parity == v
    sent_rows = stage.shape[1]
    stride = flat.shape[0] // n

    loads = [
        pltpu.make_async_copy(source, target, s_in.at[i])
        for i, (source, target) in enumerate(
            (
                (x_hbm.at[0, 0], x_ref),
                (obs_hbm.at[0], obs_ref),
                (tt_hbm, tt_ref.at[pl.ds(0, taps)]),
                (ts_hbm, ts_ref.at[pl.ds(0, taps)]),
                (th_hbm, th_ref),
            )
        )
    ]
    for load in loads[:2]:
        load.start()

    barrier = pltpu.get_barrier_semaphore()

    def greet(i, carry):
        p = partner_of(me, i, n)
        pl.semaphore_signal(barrier, inc=1, device_id=(v, p), device_id_type=MESH)
        pl.semaphore_signal(barrier, inc=1, device_id=(other, p), device_id_type=MESH)
        return carry

    lax.fori_loop(1, n, greet, 0)
    pl.semaphore_signal(barrier, inc=1, device_id=(other, me), device_id_type=MESH)
    for load in loads[2:]:
        load.start()

    tt_ref[taps:, :] = jnp.zeros((LANES - taps, channels), f32)
    ts_ref[taps:, :] = jnp.zeros((LANES - taps, channels), f32)
    plane_s[:, :LANES] = jnp.zeros((n, LANES), bf16)
    plane_s[:, LANES + width :] = jnp.zeros((n, LANES), bf16)
    if depth > taps * n:
        pst[taps * n :, :] = jnp.zeros((depth - taps * n, width), bf16)

    def put(ref, i, stride, value):
        ref[pl.ds(i, n, stride=stride), :] = value

    def take(ref, i, stride):
        return ref[pl.ds(i, n, stride=stride), :]

    def tile_of(ref, i):
        return ref[:, i * LANES : (i + 1) * LANES].astype(f32) if 0 <= i < nt else None

    lane = lane_of((n, LANES))
    mark = jnp.full((n, LANES), d_hbm[0, 0], jnp.int32)
    put(flat, nt + most, stride, mark.astype(f32))
    put(flat, nt + most + 1, stride, jnp.zeros((n, LANES), f32))
    for load in loads[:2]:
        load.wait()

    def tile_of(ref, i):
        return ref[:, i * LANES : (i + 1) * LANES].astype(f32) if 0 <= i < nt else None

    late = shifter(lambda j: tile_of(x_ref, j - most), MAXD - mark, most)
    for i in range(nt):
        put(flat, i, stride, tile_of(obs_ref, i) - late(i))
    for i in range(most):
        put(flat, nt + i, stride, tile_of(x_ref, nt - most + i))
    stage[...] = flat[...].reshape(n, stride, LANES)[:, :sent_rows].astype(bf16)
    for i in range(nt // 2):
        part = pl.ds(pl.multiple_of(v * (width // 2) + i * LANES, LANES), LANES)
        put(flat3, i, nt // 2, obs_ref[:, part].astype(f32))
    stage3[...] = flat3[...].reshape(n, nt // 2, LANES).astype(bf16)

    pl.semaphore_wait(barrier, 2 * n - 1)

    def hand(src, dst, send_sem, recv_sem, vessel, p):
        return pltpu.make_async_remote_copy(
            src_ref=src,
            dst_ref=dst,
            send_sem=send_sem,
            recv_sem=recv_sem,
            device_id=(vessel, p),
            device_id_type=MESH,
        )

    slot = v * half + me // 2

    def payload(p):
        return hand(stage.at[p], rbuf.at[slot], s_pay, r_pay, parity, p)

    def later(p):
        return hand(stage3.at[p], rbuf3.at[slot], s_late, r_late, parity, p)

    def result(vessel, i):
        return hand(stage2.at[vessel * half + i], rbuf2.at[me], s_out, r_out, vessel, 2 * i + v)

    def settle(src, dst, send_sem, recv_sem, wait):
        for own, count in ((mine, n - 1), (jnp.logical_not(mine), n)):

            @pl.when(own)
            def _(count=count):
                wait(hand(src.at[pl.ds(0, count)], dst.at[pl.ds(0, count)], send_sem, recv_sem, other, me))

    def arrived(copy):
        copy.wait_recv()

    def gone(copy):
        copy.wait_send()

    def send(i, carry):
        payload(partner_of(me, i, n)).start()
        return carry

    lax.fori_loop(1, n, send, 0)

    @pl.when(mine)
    def _():
        rbuf[slot] = stage[me]

    @pl.when(jnp.logical_not(mine))
    def _():
        payload(me).start()

    def build(q, carry):
        row_ch = q * group + lax.broadcasted_iota(jnp.int32, (rows, channels), 0) // n
        pick = row_ch == lax.broadcasted_iota(jnp.int32, (rows, channels), 1)
        pick_f = pick.astype(f32)
        spread = functools.partial(
            lax.dot_general,
            dimension_numbers=(((1,), (1,)), ((), ())),
            precision=lax.Precision.HIGHEST,
            preferred_element_type=f32,
        )
        tt = spread(pick_f, tt_ref[...])
        ts = spread(pick_f, ts_ref[...])
        th_s[q] = jnp.broadcast_to(jnp.sum(jnp.where(pick, th_ref[...], 0.0), axis=1, keepdims=True), (rows, LANES)).astype(bf16)
        row = lax.broadcasted_iota(jnp.int32, (rows, LANES), 0)
        for c in range(depth // LANES):
            col = c * LANES + lax.broadcasted_iota(jnp.int32, (rows, LANES), 1)
            tap = col // n
            to, at = lax.rem(col, n), lax.rem(row, n)
            apart = to - at + REACH
            reached = (apart >= 0) & (apart < taps) & ((to >= half) == (at >= half)) & (tap < taps)
            a = jnp.take_along_axis(tt, jnp.minimum(tap, taps), axis=1, mode="promise_in_bounds")
            b = jnp.take_along_axis(ts, jnp.clip(apart, 0, taps), axis=1, mode="promise_in_bounds")
            m = jnp.where(reached, a * b, 0.0)
            m_s[q, :, c * LANES : (c + 1) * LANES] = m.astype(bf16)
            mt_s[q, c * LANES : (c + 1) * LANES, :] = m.T.astype(bf16)
        return carry

    for load in loads[2:]:
        load.wait()
    if chunks == 1:
        build(0, 0)
    else:
        lax.fori_loop(0, chunks, build, 0)

    def send_later(i, carry):
        later(partner_of(me, i, n)).start()
        return carry

    lax.fori_loop(1, n, send_later, 0)

    @pl.when(mine)
    def _():
        rbuf3[slot] = stage3[me]

    @pl.when(jnp.logical_not(mine))
    def _():
        later(me).start()

    def shrink(y, q):
        y = y.astype(bf16)
        th = across(th_s[q], y.shape[1])
        return y - jnp.minimum(jnp.maximum(y, -th), th)

    def forward(q, start, stop):
        return jnp.dot(m_s[q], pst[:, start:stop], preferred_element_type=f32)

    def back(q, y):
        return jnp.dot(mt_s[q], shrink(y, q), preferred_element_type=f32)

    def filter_columns(start, stop):
        g_s[:, start:stop] = back(0, forward(0, start, stop))
        if chunks > 1:

            def more(q, carry):
                g_s[:, start:stop] += back(q, forward(q, start, stop))
                return carry

            lax.fori_loop(1, chunks, more, 0)

    def stack_taps(start, stop):
        piece = plane_s[:, start : stop + 2 * LANES]
        extent = piece.shape[1]
        for k in range(taps):
            step = (k - REACH) * TIME_SPACING
            moved = piece if step == 0 else pltpu.roll(piece, (extent - step) % extent, 1)
            pst[k * n : (k + 1) * n, start:stop] = moved[:, LANES : LANES + stop - start]

    def collector():
        @functools.cache
        def rolled(k, i):
            step = (k - REACH) * TIME_SPACING
            return pltpu.roll(g_s[k * n : (k + 1) * n, i * LANES : (i + 1) * LANES], step % LANES, 1)

        def value(i):
            total = g_s[REACH * n : (REACH + 1) * n, i * LANES : (i + 1) * LANES]
            for k in range(taps):
                step = (k - REACH) * TIME_SPACING
                if step == 0:
                    continue
                aside = i - 1 if step > 0 else i + 1
                there = rolled(k, aside) if 0 <= aside < nt else jnp.zeros((n, LANES), f32)
                inside = lane >= step if step > 0 else lane < LANES + step
                total = total + jnp.where(inside, rolled(k, i), there)
            return total.astype(bf16).astype(f32)

        return value

    def store_plane(i, value):
        plane_s[:, LANES + i * LANES : LANES + (i + 1) * LANES] = value.astype(bf16)

    cut = nt - most
    def before_end(i, delay):
        return i * LANES + lane + delay < width

    def run(plane, done):
        collect = collector()
        for i in range(nt):
            plane(i)
        stack_taps(0, width)
        filter_columns(0, width)
        for i in range(nt):
            done(i, collect(i))

    settle(stage, rbuf, s_pay, r_pay, arrived)
    for i in range(n):
        flat[i * stride : i * stride + sent_rows, :] = rbuf[i].astype(f32)

    def swapped(value):
        return jnp.concatenate([value[half:], value[:half]], axis=0)

    def observed(i):
        if i >= nt:
            return None
        first = (0 if i < nt // 2 else half) * (nt // 2) + i % (nt // 2)
        piece = flat3[pl.ds(first, half, stride=nt // 2), :]
        return jnp.concatenate([piece, piece], axis=0)

    delay = take(flat, nt + most, stride).astype(jnp.int32)
    ahead = shifter(lambda j: swapped(take(flat, j, stride)) if j < nt else None, delay, most)

    def plane_one(i):
        value = ahead(i)
        store_plane(i, value if i < cut else jnp.where(before_end(i, delay), value, take(flat, nt + i - cut, stride)))

    held = {}
    run(plane_one, held.__setitem__)

    settle(stage3, rbuf3, s_late, r_late, arrived)
    flat3[...] = rbuf3[...].astype(f32).reshape(n * (nt // 2), LANES)
    seen = shifter(observed, delay, most)
    apart = delay - swapped(delay) + MAXD
    again = shifter(lambda j: swapped(held[j - most]) if 0 <= j - most < nt else None, apart, 2 * most)

    def plane_two(i):
        value = seen(i) - again(i)
        store_plane(i, value if i < cut else jnp.where(before_end(i, delay), value, held[i]))

    run(plane_two, lambda i, value: put(flat2, i, nt, value))

    stage2[...] = flat2[...].reshape(n, nt, LANES).astype(bf16)
    place = me // 2

    def send_back(t, carry):
        i = place ^ (half - t) if half & (half - 1) == 0 else lax.rem(place + t, half)
        result(v, i).start()
        result(other, i).start()
        return carry

    lax.fori_loop(1, half, send_back, 0)
    result(other, place).start()

    @pl.when(mine)
    def _():
        rbuf2[me] = stage2[slot]

    @pl.when(jnp.logical_not(mine))
    def _():
        result(v, place).start()

    settle(stage, rbuf, s_pay, r_pay, gone)
    settle(stage3, rbuf3, s_late, r_late, gone)
    settle(stage2, rbuf2, s_out, r_out, arrived)
    flat2[...] = rbuf2[...].astype(f32).reshape(n * nt, LANES)
    for i in range(nt):
        out_ref[0, 0, :, i * LANES : (i + 1) * LANES] = take(flat2, i, nt).astype(bf16)
    settle(stage2, rbuf2, s_out, r_out, gone)


def per_device(n, observed, estimate, delays, taps_time, taps_shot, thresh):
    receivers, width = observed.shape[1:]
    channels, taps = taps_time.shape
    assert observed.shape[0] == 1 and receivers == n and n % 2 == 0 and width % (2 * LANES) == 0
    group = max(1, min(channels, 256 // n))
    chunks = channels // group
    rows = group * n
    depth = -(-taps * n // LANES) * LANES
    nt = width // LANES
    sent_rows = nt + MAXD // LANES + 2
    stride = -(-sent_rows // 8) * 8
    bf16, f32 = jnp.bfloat16, jnp.float32
    vmem = pl.BlockSpec(memory_space=pltpu.VMEM)
    dma = pltpu.SemaphoreType.DMA
    operands = (estimate, observed, delays, taps_time.T, taps_shot.T, thresh.reshape(1, channels))
    operands = [o if o is delays else pltpu.with_memory_space_constraint(o, pltpu.HBM) for o in operands]
    return pl.pallas_call(
        functools.partial(kernel, (n, width, channels, taps, chunks, rows, depth)),
        out_shape=pltpu.VMEM(estimate.shape, bf16),
        in_specs=[pl.BlockSpec(memory_space=pltpu.SMEM if i == 2 else pl.ANY) for i in range(6)],
        out_specs=vmem,
        scratch_shapes=[
            pltpu.VMEM((n, width), bf16),
            pltpu.VMEM((n, width), bf16),
            pltpu.VMEM((LANES, channels), f32),
            pltpu.VMEM((LANES, channels), f32),
            pltpu.VMEM((1, channels), f32),
            dma((5,)),
            pltpu.VMEM((n * stride, LANES), f32),
            pltpu.VMEM((n, sent_rows, LANES), bf16),
            pltpu.VMEM((n, sent_rows, LANES), bf16),
            pltpu.VMEM((n * nt, LANES), f32),
            pltpu.VMEM((n, nt, LANES), bf16),
            pltpu.VMEM((n, nt, LANES), bf16),
            pltpu.VMEM((n * (nt // 2), LANES), f32),
            pltpu.VMEM((n, nt // 2, LANES), bf16),
            pltpu.VMEM((n, nt // 2, LANES), bf16),
            pltpu.VMEM((chunks, rows, depth), bf16),
            pltpu.VMEM((chunks, depth, rows), bf16),
            pltpu.VMEM((chunks, rows, LANES), bf16),
            pltpu.VMEM((n, width + 2 * LANES), bf16),
            pltpu.VMEM((depth, width), bf16),
            pltpu.VMEM((depth, width), f32),
        ]
        + [dma(())] * 6,
        compiler_params=pltpu.CompilerParams(collective_id=0, has_side_effects=True, vmem_limit_bytes=48 << 20),
    )(*operands)


def solution(mesh):
    return jax.shard_map(
        functools.partial(per_device, mesh.shape["gather"]),
        mesh=mesh,
        in_specs=(
            P("gather", None, None),
            P("vessel", "gather", None, None),
            P("vessel", "gather"),
            P(),
            P(),
            P(),
        ),
        out_specs=P("vessel", "gather", None, None),
        check_vma=False,
    )
```

```python
import functools

import jax
import jax.numpy as jnp
from jax import lax
from jax.experimental import pallas as pl
from jax.experimental.pallas import tpu as pltpu
from jax.sharding import PartitionSpec as P

TIME_SPACING = 4
MAXD = 256
ITERS = 2
LANES = 128
REACH = 3

MESH = pl.DeviceIdType.MESH


def partner_of(me, i, n):
    return me ^ (n - i) if n & (n - 1) == 0 else lax.rem(me + i, n)


def across(column, extent):
    return jnp.concatenate([column] * (extent // LANES), axis=1)


def lane_of(shape):
    return lax.broadcasted_iota(jnp.int32, shape, 1)


def shifter(tile, amount, most):
    within = amount & (LANES - 1)
    whole = amount >> (LANES.bit_length() - 1)
    reach = lane_of(amount.shape) + within
    index = reach & (LANES - 1)
    wrapped = reach >= LANES
    steps = []
    while 1 << len(steps) < most:
        steps.append((whole & (1 << len(steps))) != 0)
    farthest = whole == most

    def pick(mask, a, b):
        if a is None and b is None:
            return None
        zero = jnp.zeros(amount.shape, jnp.float32)
        return jnp.where(mask, zero if a is None else a, zero if b is None else b)

    @functools.cache
    def turned(j):
        t = tile(j)
        return None if t is None else jnp.take_along_axis(t, index, axis=1, mode="promise_in_bounds")

    @functools.cache
    def level(depth, j):
        if depth == 0:
            return pick(wrapped, turned(j + 1), turned(j))
        return pick(steps[depth - 1], level(depth - 1, j + (1 << (depth - 1))), level(depth - 1, j))

    def value(i):
        found = pick(farthest, turned(i + most), level(len(steps), i))
        return jnp.zeros(amount.shape, jnp.float32) if found is None else found

    return value


def kernel(
    dims,
    x_hbm,
    obs_hbm,
    d_hbm,
    tt_hbm,
    ts_hbm,
    th_hbm,
    out_ref,
    x_ref,
    obs_ref,
    tt_ref,
    ts_ref,
    th_ref,
    s_in,
    flat,
    stage,
    rbuf,
    flat2,
    stage2,
    rbuf2,
    flat3,
    stage3,
    rbuf3,
    m_s,
    mt_s,
    th_s,
    plane_s,
    pst,
    g_s,
    s_pay,
    r_pay,
    s_late,
    r_late,
    s_out,
    r_out,
):
    n, width, channels, taps, chunks, rows, depth = dims
    v = lax.axis_index("vessel")
    me = lax.axis_index("gather")
    other = 1 - v
    nt = width // LANES
    group = rows // n
    f32, bf16 = jnp.float32, jnp.bfloat16
    half = n // 2
    most = MAXD // LANES
    parity = lax.rem(me, 2)
    mine = parity == v
    sent_rows = stage.shape[1]
    stride = flat.shape[0] // n

    loads = [
        pltpu.make_async_copy(source, target, s_in.at[i])
        for i, (source, target) in enumerate(
            (
                (x_hbm.at[0, 0], x_ref),
                (obs_hbm.at[0], obs_ref),
                (tt_hbm, tt_ref.at[pl.ds(0, taps)]),
                (ts_hbm, ts_ref.at[pl.ds(0, taps)]),
                (th_hbm, th_ref),
            )
        )
    ]
    for load in loads[:2]:
        load.start()

    barrier = pltpu.get_barrier_semaphore()

    def greet(i, carry):
        p = partner_of(me, i, n)
        pl.semaphore_signal(barrier, inc=1, device_id=(v, p), device_id_type=MESH)
        pl.semaphore_signal(barrier, inc=1, device_id=(other, p), device_id_type=MESH)
        return carry

    lax.fori_loop(1, n, greet, 0)
    pl.semaphore_signal(barrier, inc=1, device_id=(other, me), device_id_type=MESH)
    for load in loads[2:]:
        load.start()

    tt_ref[taps:, :] = jnp.zeros((LANES - taps, channels), f32)
    ts_ref[taps:, :] = jnp.zeros((LANES - taps, channels), f32)
    plane_s[:, :LANES] = jnp.zeros((n, LANES), bf16)
    plane_s[:, LANES + width :] = jnp.zeros((n, LANES), bf16)
    if depth > taps * n:
        pst[taps * n :, :] = jnp.zeros((depth - taps * n, width), bf16)

    def put(ref, i, stride, value):
        ref[pl.ds(i, n, stride=stride), :] = value

    def take(ref, i, stride):
        return ref[pl.ds(i, n, stride=stride), :]

    def tile_of(ref, i):
        return ref[:, i * LANES : (i + 1) * LANES].astype(f32) if 0 <= i < nt else None

    lane = lane_of((n, LANES))
    mark = jnp.full((n, LANES), d_hbm[0, 0], jnp.int32)
    put(flat, nt + most, stride, mark.astype(f32))
    put(flat, nt + most + 1, stride, jnp.zeros((n, LANES), f32))
    for load in loads[:2]:
        load.wait()

    def tile_of(ref, i):
        return ref[:, i * LANES : (i + 1) * LANES].astype(f32) if 0 <= i < nt else None

    late = shifter(lambda j: tile_of(x_ref, j - most), MAXD - mark, most)
    for i in range(nt):
        put(flat, i, stride, tile_of(obs_ref, i) - late(i))
    for i in range(most):
        put(flat, nt + i, stride, tile_of(x_ref, nt - most + i))
    stage[...] = flat[...].reshape(n, stride, LANES)[:, :sent_rows].astype(bf16)
    for i in range(nt // 2):
        part = pl.ds(pl.multiple_of(v * (width // 2) + i * LANES, LANES), LANES)
        put(flat3, i, nt // 2, obs_ref[:, part].astype(f32))
    stage3[...] = flat3[...].reshape(n, nt // 2, LANES).astype(bf16)

    pl.semaphore_wait(barrier, 2 * n - 1)

    def hand(src, dst, send_sem, recv_sem, vessel, p):
        return pltpu.make_async_remote_copy(
            src_ref=src,
            dst_ref=dst,
            send_sem=send_sem,
            recv_sem=recv_sem,
            device_id=(vessel, p),
            device_id_type=MESH,
        )

    slot = v * half + me // 2

    def payload(p):
        return hand(stage.at[p], rbuf.at[slot], s_pay, r_pay, parity, p)

    def later(p):
        return hand(stage3.at[p], rbuf3.at[slot], s_late, r_late, parity, p)

    def result(vessel, i):
        return hand(stage2.at[vessel * half + i], rbuf2.at[me], s_out, r_out, vessel, 2 * i + v)

    def settle(src, dst, send_sem, recv_sem, wait):
        for own, count in ((mine, n - 1), (jnp.logical_not(mine), n)):

            @pl.when(own)
            def _(count=count):
                wait(hand(src.at[pl.ds(0, count)], dst.at[pl.ds(0, count)], send_sem, recv_sem, other, me))

    def arrived(copy):
        copy.wait_recv()

    def gone(copy):
        copy.wait_send()

    def send(i, carry):
        payload(partner_of(me, i, n)).start()
        return carry

    lax.fori_loop(1, n, send, 0)

    @pl.when(mine)
    def _():
        rbuf[slot] = stage[me]

    @pl.when(jnp.logical_not(mine))
    def _():
        payload(me).start()

    def build(q, carry):
        row_ch = q * group + lax.broadcasted_iota(jnp.int32, (rows, channels), 0) // n
        pick = row_ch == lax.broadcasted_iota(jnp.int32, (rows, channels), 1)
        pick_f = pick.astype(f32)
        spread = functools.partial(
            lax.dot_general,
            dimension_numbers=(((1,), (1,)), ((), ())),
            precision=lax.Precision.HIGHEST,
            preferred_element_type=f32,
        )
        tt = spread(pick_f, tt_ref[...])
        ts = spread(pick_f, ts_ref[...])
        th_s[q] = jnp.broadcast_to(jnp.sum(jnp.where(pick, th_ref[...], 0.0), axis=1, keepdims=True), (rows, LANES)).astype(bf16)
        row = lax.broadcasted_iota(jnp.int32, (rows, LANES), 0)
        for c in range(depth // LANES):
            col = c * LANES + lax.broadcasted_iota(jnp.int32, (rows, LANES), 1)
            tap = col // n
            to, at = lax.rem(col, n), lax.rem(row, n)
            apart = to - at + REACH
            reached = (apart >= 0) & (apart < taps) & ((to >= half) == (at >= half)) & (tap < taps)
            a = jnp.take_along_axis(tt, jnp.minimum(tap, taps), axis=1, mode="promise_in_bounds")
            b = jnp.take_along_axis(ts, jnp.clip(apart, 0, taps), axis=1, mode="promise_in_bounds")
            m = jnp.where(reached, a * b, 0.0)
            m_s[q, :, c * LANES : (c + 1) * LANES] = m.astype(bf16)
            mt_s[q, c * LANES : (c + 1) * LANES, :] = m.T.astype(bf16)
        return carry

    for load in loads[2:]:
        load.wait()
    if chunks == 1:
        build(0, 0)
    else:
        lax.fori_loop(0, chunks, build, 0)

    pl.delay(300)
    def send_later(i, carry):
        later(partner_of(me, i, n)).start()
        return carry

    lax.fori_loop(1, n, send_later, 0)

    @pl.when(mine)
    def _():
        rbuf3[slot] = stage3[me]

    @pl.when(jnp.logical_not(mine))
    def _():
        later(me).start()

    def shrink(y, q):
        y = y.astype(bf16)
        th = across(th_s[q], y.shape[1])
        return y - jnp.minimum(jnp.maximum(y, -th), th)

    def forward(q, start, stop):
        return jnp.dot(m_s[q], pst[:, start:stop], preferred_element_type=f32)

    def back(q, y):
        return jnp.dot(mt_s[q], shrink(y, q), preferred_element_type=f32)

    def filter_columns(start, stop):
        g_s[:, start:stop] = back(0, forward(0, start, stop)).astype(g_s.dtype)
        if chunks > 1:

            def more(q, carry):
                g_s[:, start:stop] += back(q, forward(q, start, stop))
                return carry

            lax.fori_loop(1, chunks, more, 0)

    def stack_taps(start, stop):
        piece = plane_s[:, start : stop + 2 * LANES]
        extent = piece.shape[1]
        for k in range(taps):
            step = (k - REACH) * TIME_SPACING
            moved = piece if step == 0 else pltpu.roll(piece, (extent - step) % extent, 1)
            pst[k * n : (k + 1) * n, start:stop] = moved[:, LANES : LANES + stop - start]

    def collector():
        @functools.cache
        def rolled(k, i):
            step = (k - REACH) * TIME_SPACING
            return pltpu.roll(g_s[k * n : (k + 1) * n, i * LANES : (i + 1) * LANES], step % LANES, 1)

        def value(i):
            total = g_s[REACH * n : (REACH + 1) * n, i * LANES : (i + 1) * LANES].astype(f32)
            for k in range(taps):
                step = (k - REACH) * TIME_SPACING
                if step == 0:
                    continue
                aside = i - 1 if step > 0 else i + 1
                there = rolled(k, aside) if 0 <= aside < nt else jnp.zeros((n, LANES), g_s.dtype)
                inside = lane >= step if step > 0 else lane < LANES + step
                total = total + jnp.where(inside, rolled(k, i), there).astype(f32)
            return total.astype(bf16).astype(f32)

        return value

    def store_plane(i, value):
        plane_s[:, LANES + i * LANES : LANES + (i + 1) * LANES] = value.astype(bf16)

    cut = nt - most
    def before_end(i, delay):
        return i * LANES + lane + delay < width

    def run(plane, done):
        collect = collector()
        for i in range(nt):
            plane(i)
        stack_taps(0, width)
        if chunks > 1:
            filter_columns(0, width)
            for i in range(nt):
                done(i, collect(i))
            return
        middle = nt // 2 * LANES
        spans = ((0, middle), (middle, width))
        passed = [forward(0, *span) for span in spans]
        g_s[:, :middle] = back(0, passed[0]).astype(g_s.dtype)
        for i in range(nt // 2 - 1):
            done(i, collect(i))
        g_s[:, middle:] = back(0, passed[1]).astype(g_s.dtype)
        for i in range(nt // 2 - 1, nt):
            done(i, collect(i))

    settle(stage, rbuf, s_pay, r_pay, arrived)
    for i in range(n):
        flat[i * stride : i * stride + sent_rows, :] = rbuf[i].astype(f32)

    def swapped(value):
        return jnp.concatenate([value[half:], value[:half]], axis=0)

    def observed(i):
        if i >= nt:
            return None
        first = (0 if i < nt // 2 else half) * (nt // 2) + i % (nt // 2)
        piece = flat3[pl.ds(first, half, stride=nt // 2), :]
        return jnp.concatenate([piece, piece], axis=0)

    delay = take(flat, nt + most, stride).astype(jnp.int32)
    ahead = shifter(lambda j: swapped(take(flat, j, stride)) if j < nt else None, delay, most)

    def plane_one(i):
        value = ahead(i)
        store_plane(i, value if i < cut else jnp.where(before_end(i, delay), value, take(flat, nt + i - cut, stride)))

    held = {}
    run(plane_one, held.__setitem__)

    settle(stage3, rbuf3, s_late, r_late, arrived)
    flat3[...] = rbuf3[...].astype(f32).reshape(n * (nt // 2), LANES)
    seen = shifter(observed, delay, most)
    apart = delay - swapped(delay) + MAXD
    again = shifter(lambda j: swapped(held[j - most]) if 0 <= j - most < nt else None, apart, 2 * most)

    def plane_two(i):
        value = seen(i) - again(i)
        store_plane(i, value if i < cut else jnp.where(before_end(i, delay), value, held[i]))

    run(plane_two, lambda i, value: put(flat2, i, nt, value))

    stage2[...] = flat2[...].reshape(n, nt, LANES).astype(bf16)
    place = me // 2

    def send_back(t, carry):
        i = place ^ (half - t) if half & (half - 1) == 0 else lax.rem(place + t, half)
        result(v, i).start()
        result(other, i).start()
        return carry

    lax.fori_loop(1, half, send_back, 0)
    result(other, place).start()

    @pl.when(mine)
    def _():
        rbuf2[me] = stage2[slot]

    @pl.when(jnp.logical_not(mine))
    def _():
        result(v, place).start()

    settle(stage, rbuf, s_pay, r_pay, gone)
    settle(stage3, rbuf3, s_late, r_late, gone)
    settle(stage2, rbuf2, s_out, r_out, arrived)
    flat2[...] = rbuf2[...].astype(f32).reshape(n * nt, LANES)
    for i in range(nt):
        out_ref[0, 0, :, i * LANES : (i + 1) * LANES] = take(flat2, i, nt).astype(bf16)
    settle(stage2, rbuf2, s_out, r_out, gone)


def per_device(n, observed, estimate, delays, taps_time, taps_shot, thresh):
    receivers, width = observed.shape[1:]
    channels, taps = taps_time.shape
    assert observed.shape[0] == 1 and receivers == n and n % 2 == 0 and width % (2 * LANES) == 0
    group = max(1, min(channels, 256 // n))
    chunks = channels // group
    rows = group * n
    depth = -(-taps * n // LANES) * LANES
    nt = width // LANES
    sent_rows = nt + MAXD // LANES + 2
    stride = -(-sent_rows // 8) * 8
    bf16, f32 = jnp.bfloat16, jnp.float32
    vmem = pl.BlockSpec(memory_space=pltpu.VMEM)
    dma = pltpu.SemaphoreType.DMA
    operands = (estimate, observed, delays, taps_time.T, taps_shot.T, thresh.reshape(1, channels))
    operands = [o if o is delays else pltpu.with_memory_space_constraint(o, pltpu.HBM) for o in operands]
    return pl.pallas_call(
        functools.partial(kernel, (n, width, channels, taps, chunks, rows, depth)),
        out_shape=pltpu.VMEM(estimate.shape, bf16),
        in_specs=[pl.BlockSpec(memory_space=pltpu.SMEM if i == 2 else pl.ANY) for i in range(6)],
        out_specs=vmem,
        scratch_shapes=[
            pltpu.VMEM((n, width), bf16),
            pltpu.VMEM((n, width), bf16),
            pltpu.VMEM((LANES, channels), f32),
            pltpu.VMEM((LANES, channels), f32),
            pltpu.VMEM((1, channels), f32),
            dma((5,)),
            pltpu.VMEM((n * stride, LANES), f32),
            pltpu.VMEM((n, sent_rows, LANES), bf16),
            pltpu.VMEM((n, sent_rows, LANES), bf16),
            pltpu.VMEM((n * nt, LANES), f32),
            pltpu.VMEM((n, nt, LANES), bf16),
            pltpu.VMEM((n, nt, LANES), bf16),
            pltpu.VMEM((n * (nt // 2), LANES), f32),
            pltpu.VMEM((n, nt // 2, LANES), bf16),
            pltpu.VMEM((n, nt // 2, LANES), bf16),
            pltpu.VMEM((chunks, rows, depth), bf16),
            pltpu.VMEM((chunks, depth, rows), bf16),
            pltpu.VMEM((chunks, rows, LANES), bf16),
            pltpu.VMEM((n, width + 2 * LANES), bf16),
            pltpu.VMEM((depth, width), bf16),
            pltpu.VMEM((depth, width), bf16 if chunks == 1 else f32),
        ]
        + [dma(())] * 6,
        compiler_params=pltpu.CompilerParams(collective_id=0, has_side_effects=True, vmem_limit_bytes=48 << 20),
    )(*operands)


def solution(mesh):
    return jax.shard_map(
        functools.partial(per_device, mesh.shape["gather"]),
        mesh=mesh,
        in_specs=(
            P("gather", None, None),
            P("vessel", "gather", None, None),
            P("vessel", "gather"),
            P(),
            P(),
            P(),
        ),
        out_specs=P("vessel", "gather", None, None),
        check_vma=False,
    )
```
